512 devices in a mesh: doc: 4 (over x), topic: 16 (over z, core), vocab: 8 (over y).
Axes of the slice: x: 4, y: 8, z: 8, core: 2. Of those that a mesh axis runs over, the one named last changes fastest.
Arguments:
- doc_topics: bfloat16 [2048, 16384], P('doc', 'topic'), may hold values from 0 to 1, as said below
- word_logits: bfloat16 [2048, 16384], P('vocab', 'topic'), may hold values from -6 to 11
- log_norm: float32 [16384], P('topic'), may hold values from 12 to 16
- tile_doc: int32 [512], P(('doc', 'vocab')), may hold values from 0 to 3, as said below
- tile_word: int32 [512], P(('doc', 'vocab')), may hold values from 0 to 3
- word_counts: int32 [512, 64, 128], P(('doc', 'vocab')), may hold values from 0 to 3, as said below
Outputs:
- doc_topic_grad: float32 [2048, 16384], P('doc', ('topic', 'vocab'))
- word_logit_grad: bfloat16 [2048, 16384], P('vocab', 'topic')
The draws below stay inside these ranges and needn't reach their ends.
Inputs may be any that keep to these rules, and one draw needn't show every extreme that they name: `doc_topics`: each document's row is a softmax over the 16384 topics. Within the 16 slots of one doc and vocab index pair no (tile_doc, tile_word) pair repeats. `word_counts`: A slot whose counts are all zero is empty; occupied slots come first in each pair's list, and in every draw some pair has all 16 slots occupied.
All inputs are finite; a program needn't handle non-finite values.
Results may differ from the reference program's by a relative error of at most 0.018.
Values may be sent and summed in bfloat16 or wider, within the bound.
A program may use at most 64 MiB of HBM per device.

```python
import jax
import jax.numpy as jnp
from jax import lax

K = 16384
DOC_TILE = 128
WORD_TILE = 64
DB_DEV = 4
WB_DEV = 4
TILES_DEV = 16
NDOC = 2048
VWIN = 2048
ALL_TILES = 512
N_DOC = 4
N_VOCAB = 8


def tile_layout(key):
    base = jax.random.fold_in(key, 7)
    pair_total = ALL_TILES // TILES_DEV
    places_all = DB_DEV * WB_DEV
    keys = jax.random.split(base, pair_total)

    def pick_places(one_key):
        return jax.random.permutation(one_key, places_all)[:TILES_DEV]
    places = jax.vmap(pick_places)(keys).astype(jnp.int32)
    occupied = jax.random.randint(jax.random.fold_in(base, 11), (pair_total,), TILES_DEV // 4, TILES_DEV + 1)
    fullest = jax.random.randint(jax.random.fold_in(base, 13), (), 0, pair_total)
    occupied = jnp.where(jnp.arange(pair_total) == fullest, TILES_DEV, occupied)
    return (places, occupied)


def draw_tile_doc(key, part):
    places, occupied = tile_layout(key)
    return (places // WB_DEV).reshape(-1).astype(jnp.int32)


def draw_tile_word(key, part):
    places, occupied = tile_layout(key)
    return (places % WB_DEV).reshape(-1).astype(jnp.int32)


def draw_word_counts(key, part):
    places, occupied = tile_layout(key)
    live_slots = (jnp.arange(TILES_DEV)[None, :] < occupied[:, None]).reshape(-1).astype(jnp.int32)
    values = jax.random.randint(jax.random.fold_in(key, 21), (ALL_TILES, WORD_TILE, DOC_TILE), 1, 4)
    present = (jax.random.randint(jax.random.fold_in(key, 23), (ALL_TILES, WORD_TILE, DOC_TILE), 0, 3) == 0).astype(jnp.int32)
    return (values * present * live_slots[:, None, None]).astype(jnp.int32)


def draw_doc_topics(key, part):
    base = jax.random.fold_in(key, 31)
    spread_draw = jnp.clip(jax.random.normal(base, (NDOC, K), jnp.float32), -6.0, 6.0)
    logits = 3.0 * spread_draw
    return jax.nn.softmax(logits, axis=-1).astype(jnp.bfloat16)


def draw_word_logits(key, part):
    base = jax.random.fold_in(key, 41)
    raised = (jax.random.randint(jax.random.fold_in(base, 5), (VWIN, K), 0, 32) == 0).astype(jnp.float32)
    noise = jnp.clip(jax.random.normal(base, (VWIN, K), jnp.float32), -6.0, 6.0)
    lift = 4.0
    return (noise + lift * raised).astype(jnp.bfloat16)


def levels(own_key, shape, pieces, least, top_value):
    def one(dim, parts):
        heights = jax.random.uniform(jax.random.fold_in(jax.random.fold_in(own_key, 6), dim), (parts,), jnp.float32, least / len(pieces), top_value / len(pieces))
        return jnp.repeat(jnp.exp(heights), shape[dim] // parts).reshape((-1,) + (1,) * (len(shape) - dim - 1))

    loudness = one(*pieces[0])
    for cut in pieces[1:]:
        loudness = loudness * one(*cut)
    return loudness


def setup_inputs(seed: int = 0) -> dict:
    splits = jax.random.split(jax.random.key(seed), 7)
    return {
        "doc_topics": draw_doc_topics(jax.random.fold_in(splits[6], 71), 0),
        "word_logits": draw_word_logits(jax.random.fold_in(splits[6], 71), 0),
        "log_norm": jnp.clip(12.0 + 4.0 * jax.random.uniform(splits[2], (K,), jnp.float32) ** levels(splits[2], (K,), ((0, 16),), -0.2, 0.2), 12.0, 16.0),
        "tile_doc": draw_tile_doc(jax.random.fold_in(splits[6], 71), 0),
        "tile_word": draw_tile_word(jax.random.fold_in(splits[6], 71), 0),
        "word_counts": draw_word_counts(jax.random.fold_in(splits[6], 71), 0),
    }


def reference(doc_topics, word_logits, log_norm, tile_doc, tile_word, word_counts):
    word_prob = jnp.exp(word_logits.astype(jnp.float32) - log_norm[None, :]).astype(jnp.bfloat16)
    doc_span = DB_DEV * DOC_TILE
    word_span = WB_DEV * WORD_TILE
    pair_total = N_DOC * N_VOCAB

    def visit_pair(state_pair, pair):
        theta_acc, beta_acc = state_pair
        shard_doc = (pair // N_VOCAB).astype(jnp.int32)
        shard_word = (pair % N_VOCAB).astype(jnp.int32)
        doc_start = (shard_doc * doc_span).astype(jnp.int32)
        word_start = (shard_word * word_span).astype(jnp.int32)
        topic_rows = lax.dynamic_slice_in_dim(doc_topics, doc_start, doc_span, 0).astype(jnp.float32)
        topic_rows = topic_rows.reshape(DB_DEV, DOC_TILE, K)
        prob_shard = lax.dynamic_slice_in_dim(word_prob, word_start, word_span, 0)
        prob_rows = prob_shard.astype(jnp.float32).reshape(WB_DEV, WORD_TILE, K)
        slot_start = (pair * TILES_DEV).astype(jnp.int32)
        doc_index = lax.dynamic_slice_in_dim(tile_doc, slot_start, TILES_DEV, 0)
        word_index = lax.dynamic_slice_in_dim(tile_word, slot_start, TILES_DEV, 0)
        counted = lax.dynamic_slice_in_dim(word_counts, slot_start, TILES_DEV, 0).astype(jnp.float32)
        doc_part = topic_rows[doc_index]
        word_part = prob_rows[word_index]
        rate = jnp.einsum('gwk,gdk->gwd', word_part, doc_part)
        ratios = (counted / (WORD_TILE * rate)).astype(jnp.bfloat16)
        ratios = lax.optimization_barrier(ratios).astype(jnp.float32)
        toward_theta = jnp.einsum('gwd,gwk->gdk', ratios, word_part)
        toward_beta = jnp.einsum('gwd,gdk->gwk', ratios, doc_part)
        theta_sum = jnp.zeros((DB_DEV, DOC_TILE, K), jnp.float32).at[doc_index].add(toward_theta)
        beta_sum = jnp.zeros((WB_DEV, WORD_TILE, K), jnp.float32).at[word_index].add(toward_beta)
        theta_part = (-theta_sum.reshape(doc_span, K)).astype(jnp.bfloat16)
        theta_part = lax.optimization_barrier(theta_part).astype(jnp.float32)
        beta_part = (-prob_shard.astype(jnp.float32) * beta_sum.reshape(word_span, K)).astype(jnp.bfloat16)
        beta_part = lax.optimization_barrier(beta_part).astype(jnp.float32)
        old_theta = lax.dynamic_slice_in_dim(theta_acc, doc_start, doc_span, 0)
        theta_acc = lax.dynamic_update_slice_in_dim(theta_acc, old_theta + theta_part, doc_start, 0)
        old_beta = lax.dynamic_slice_in_dim(beta_acc, word_start, word_span, 0)
        beta_acc = lax.dynamic_update_slice_in_dim(beta_acc, old_beta + beta_part, word_start, 0)
        return (theta_acc, beta_acc), None

    initial = (jnp.zeros((NDOC, K), jnp.float32), jnp.zeros((VWIN, K), jnp.float32))
    (theta_acc, beta_acc), _ = lax.scan(visit_pair, initial, jnp.arange(pair_total, dtype=jnp.int32))
    return theta_acc, beta_acc.astype(jnp.bfloat16)
```

```python
import functools

import jax
import jax.numpy as jnp
from jax import lax
from jax.experimental import pallas as pl
from jax.experimental.pallas import tpu as pltpu
from jax.sharding import PartitionSpec as P

MESH = pl.DeviceIdType.MESH
F32 = jnp.float32
BF16 = jnp.bfloat16
DT = 4
WT = 4
DS = 128
WS = 64
Z_ORDER = (4, 3, 5, 2, 6, 1, 7)
Z_ARRIVE = (1, 7, 2, 6, 3, 5, 4)


def kernel(
    docs_hbm, logits_hbm, norm_ref, tdoc_ref, tword_ref, counts_hbm,
    theta_hbm, beta_hbm,
    docs, logits, counts, wp,
    rate_b, c_in, z_out, z_in, rt, rt_t, rw,
    th, y_out, y_in, th_fin,
    be, x_out, x_in, be_fin,
    load_sem, c_sem, z_sem, g_sem, f_sem, y_send, y_recv, x_send, x_recv, a_send, a_recv, out_sem,
):
    i, t, l = (lax.axis_index(a) for a in ("doc", "topic", "vocab"))
    z, c = lax.div(t, 2), lax.rem(t, 2)
    other = (i, 2 * z + 1 - c, l)

    def z_peer(d):
        return (i, lax.rem(t + 2 * d, 16), l)

    def y_peer(d):
        return (i, t, lax.rem(l + d + 8, 8))

    def x_peer(d):
        return (lax.rem(i + d + 4, 4), t, l)

    loads = [
        pltpu.make_async_copy(logits_hbm, logits, load_sem.at[0]),
        pltpu.make_async_copy(docs_hbm.at[pl.ds(0, 256)], docs.at[pl.ds(0, 256)], load_sem.at[1]),
        pltpu.make_async_copy(docs_hbm.at[pl.ds(256, 256)], docs.at[pl.ds(256, 256)], load_sem.at[2]),
        pltpu.make_async_copy(counts_hbm, counts, load_sem.at[3]),
    ]
    for cp in loads:
        cp.start()

    barrier = pltpu.get_barrier_semaphore()
    partners = [other] + [z_peer(d) for d in range(1, 8)]
    partners += [y_peer(1), y_peer(-1), x_peer(1), x_peer(-1)]
    for dev in partners:
        pl.semaphore_signal(barrier, inc=1, device_id=dev, device_id_type=MESH)

    loads[0].wait()
    wp[...] = jnp.exp(logits[...].astype(F32) - norm_ref[...]).astype(BF16)
    for h in range(2):
        loads[1 + h].wait()
        rate = lax.dot_general(
            wp[...], docs[pl.ds(256 * h, 256), :], (((1,), (1,)), ((), ())), preferred_element_type=F32
        ).astype(BF16)
        for k in range(2):
            for w in range(WT):
                p = (2 * h + k) * WT + w
                rate_b[p % 2, p // 2] = rate[w * WS:(w + 1) * WS, k * DS:(k + 1) * DS]
    loads[3].wait()

    pl.semaphore_wait(barrier, len(partners))

    swap = pltpu.make_async_remote_copy(
        rate_b.at[1 - c], c_in, c_sem.at[0], c_sem.at[1], device_id=other, device_id_type=MESH
    )
    swap.start()
    slot = jnp.int32(0)
    for s in range(tdoc_ref.shape[0]):
        slot = jnp.where(tdoc_ref[s] * WT + tword_ref[s] == t, s, slot)
    count = counts[slot].astype(F32)
    swap.wait()
    z_out[...] = (rate_b[c].astype(F32) + c_in[...].astype(F32)).astype(BF16)

    scatter = []
    for d in Z_ORDER:
        cp = pltpu.make_async_remote_copy(
            z_out.at[lax.rem(z + d, 8)], z_in.at[d - 1], z_sem.at[0, d - 1], z_sem.at[1, d - 1],
            device_id=z_peer(d), device_id_type=MESH,
        )
        cp.start()
        scatter.append((d, cp))
    total = z_out[z].astype(F32)
    waits = dict(scatter)
    for d in (7, 1, 6, 2, 5, 3, 4):
        waits[d].wait_recv()
        total += z_in[d - 1].astype(F32)
    rt[t] = (-count / (WS * total)).astype(BF16)

    def fwd(src_t):
        return pltpu.make_async_remote_copy(
            rt.at[src_t], rt.at[src_t], f_sem.at[0, lax.div(src_t, 2)], f_sem.at[1, lax.div(src_t, 2)],
            device_id=other, device_id_type=MESH,
        )

    gather = {}
    for d in Z_ORDER:
        cp = pltpu.make_async_remote_copy(
            rt.at[t], rt.at[t], g_sem.at[0, d - 1], g_sem.at[1, d - 1],
            device_id=z_peer(d), device_id_type=MESH,
        )
        cp.start()
        gather[d] = cp
    mine = fwd(t)
    mine.start()
    passed = [mine]
    for d in Z_ARRIVE:
        src_t = lax.rem(t - 2 * d + 16, 16)
        pltpu.make_async_remote_copy(
            rt.at[src_t], rt.at[src_t], g_sem.at[0, d - 1], g_sem.at[1, d - 1],
            device_id=z_peer(d), device_id_type=MESH,
        ).wait_recv()
        cp = fwd(src_t)
        cp.start()
        passed.append(cp)
    for q in range(8):
        src_t = 2 * q + 1 - c
        pltpu.make_async_remote_copy(
            rt.at[src_t], rt.at[src_t], f_sem.at[0, q], f_sem.at[1, q], device_id=other, device_id_type=MESH
        ).wait_recv()

    for s in range(DT):
        tile = rt[pl.ds(s * WT, WT)].reshape(WT * WS, DS)
        rw[:, pl.ds(s * DS, DS)] = tile
        rt_t[pl.ds(s * DS, DS), :] = tile.T

    def theta(q):
        cols = pl.ds(pl.multiple_of(q * 128, 128), 128)
        th[q] = lax.dot_general(
            rt_t[...], wp[:, cols], (((1,), (0,)), ((), ())), preferred_element_type=F32
        )

    def beta(e):
        cols = pl.ds(pl.multiple_of(e * 256, 256), 256)
        be[e] = lax.dot_general(
            rw[...], docs[:, cols], (((1,), (0,)), ((), ())), preferred_element_type=F32
        )

    y_early = ((0, 1), (2, 3))
    y_order = ((2, 3, 0, 1), (0, 1, 2, 3))
    pending = []

    def y_copy(way, step, s):
        return pltpu.make_async_remote_copy(
            y_out.at[way, step, s], y_in.at[way, step, s], y_send.at[way, step, s], y_recv.at[way, step, s],
            device_id=y_peer(1 - 2 * way), device_id_type=MESH,
        )

    def y_go(way, step, s):
        sign = 1 - 2 * way
        q = lax.rem(l + sign * (4 - step) + 8, 8)
        v = th[q, pl.ds(s * DS, DS), :]
        if step > 1 or (step == 1 and s in y_early[way]):
            y_copy(way, step - 1, s).wait_recv()
            v = v + y_in[way, step - 1, s].astype(F32)
        y_out[way, step, s] = v.astype(BF16)
        cp = y_copy(way, step, s)
        cp.start()
        pending.append(cp)

    def x_copy(way, step, u):
        return pltpu.make_async_remote_copy(
            x_out.at[way, step, u], x_in.at[way, step, u], x_send.at[way, step, u], x_recv.at[way, step, u],
            device_id=x_peer(1 - 2 * way), device_id_type=MESH,
        )

    def x_go(way, step, u):
        sign = 1 - 2 * way
        e = lax.rem(i + sign * (2 - step) + 4, 4)
        v = be[e, pl.ds(u * WS, WS), :]
        if step == 1 and u in y_early[way]:
            x_copy(way, 0, u).wait_recv()
            v = v + x_in[way, 0, u].astype(F32)
        x_out[way, step, u] = v.astype(BF16)
        cp = x_copy(way, step, u)
        cp.start()
        pending.append(cp)

    def a_copy(way, e, u):
        hop = lax.rem(i - e + 4, 4)
        return pltpu.make_async_remote_copy(
            be_fin.at[e, u], be_fin.at[e, u], a_send.at[way, e, u], a_recv.at[way, e, u],
            device_id=x_peer(1 - 2 * way), device_id_type=MESH,
        )

    writes = []

    def write_beta(e, u):
        cp = pltpu.make_async_copy(
            be_fin.at[e, u],
            beta_hbm.at[pl.ds(u * WS, WS), pl.ds(pl.multiple_of(e * 256, 256), 256)],
            out_sem.at[0, e, u],
        )
        cp.start()
        writes.append(cp)

    theta(lax.rem(l + 4, 8))
    for way in range(2):
        for s in y_early[way]:
            y_go(way, 0, s)
    beta(lax.rem(i + 2, 4))
    for way in range(2):
        for u in y_early[way]:
            x_go(way, 0, u)
    theta(lax.rem(l + 3, 8))
    theta(lax.rem(l + 5, 8))
    for way in range(2):
        for s in y_early[1 - way]:
            y_go(way, 1, s)
    beta(lax.rem(i + 1, 4))
    beta(lax.rem(i + 3, 4))
    for way in range(2):
        for u in y_early[1 - way]:
            x_go(way, 1, u)
    theta(lax.rem(l + 2, 8))
    theta(lax.rem(l + 6, 8))
    beta(i)
    theta(lax.rem(l + 1, 8))
    theta(lax.rem(l + 7, 8))
    theta(l)
    for k in range(2):
        for way in range(2):
            y_go(way, 1, y_early[way][k])
        for way in range(2):
            x_go(way, 1, y_early[way][k])
    for k in range(4):
        for way in range(2):
            y_go(way, 2, y_order[way][k])

    for u in range(4):
        for way in range(2):
            x_copy(way, 1, u).wait_recv()
        v = be[i, pl.ds(u * WS, WS), :] + x_in[0, 1, u].astype(F32) + x_in[1, 1, u].astype(F32)
        w = wp[pl.ds(u * WS, WS), pl.ds(pl.multiple_of(i * 256, 256), 256)].astype(F32)
        be_fin[i, u] = (v * w).astype(BF16)
        for way in range(2):
            cp = a_copy(way, i, u)
            cp.start()
            pending.append(cp)
        write_beta(i, u)
    for k in range(4):
        for way in range(2):
            y_go(way, 3, y_order[way][k])
    for u in range(4):
        for way in range(2):
            e = lax.rem(i - (1 - 2 * way) + 4, 4)
            a_copy(way, e, u).wait_recv()
            if u in y_early[way]:
                cp = a_copy(way, e, u)
                cp.start()
                pending.append(cp)
            write_beta(e, u)
    for k in range(4):
        s = k
        for way in range(2):
            y_copy(way, 3, s).wait_recv()
        th_fin[pl.ds(s * DS, DS), :] = (
            th[l, pl.ds(s * DS, DS), :] + y_in[0, 3, s].astype(F32) + y_in[1, 3, s].astype(F32)
        )
        cp = pltpu.make_async_copy(
            th_fin.at[pl.ds(s * DS, DS)], theta_hbm.at[pl.ds(s * DS, DS)], out_sem.at[1, 0, s]
        )
        cp.start()
        writes.append(cp)
    e = lax.rem(i + 2, 4)
    for way in range(2):
        for u in y_early[way]:
            a_copy(way, e, u).wait_recv()
            write_beta(e, u)

    for cp in [waits[d] for d in Z_ORDER] + [gather[d] for d in Z_ORDER] + passed + pending:
        cp.wait_send()
    for cp in writes:
        cp.wait()


def on_device(doc_topics, word_logits, log_norm, tile_doc, tile_word, word_counts):
    n_docs, width = doc_topics.shape
    n_words = word_logits.shape[0]
    hbm = pl.BlockSpec(memory_space=pltpu.HBM)
    vmem = pl.BlockSpec(memory_space=pltpu.VMEM)
    smem = pl.BlockSpec(memory_space=pltpu.SMEM)
    V, D = pltpu.VMEM, pltpu.SemaphoreType.DMA
    return pl.pallas_call(
        kernel,
        out_shape=(
            jax.ShapeDtypeStruct((n_docs, 128), F32),
            jax.ShapeDtypeStruct((n_words, width), BF16),
        ),
        in_specs=[hbm, hbm, vmem, smem, smem, hbm],
        out_specs=(hbm, hbm),
        scratch_shapes=[
            V((n_docs, width), BF16),
            V((n_words, width), BF16),
            V(word_counts.shape, jnp.int32),
            V((n_words, width), BF16),
            V((2, 8, WS, DS), BF16),
            V((8, WS, DS), BF16),
            V((8, WS, DS), BF16),
            V((7, WS, DS), BF16),
            V((16, WS, DS), BF16),
            V((n_docs, n_words), BF16),
            V((n_words, n_docs), BF16),
            V((8, n_docs, 128), F32),
            V((2, 4, 4, DS, 128), BF16),
            V((2, 4, 4, DS, 128), BF16),
            V((n_docs, 128), F32),
            V((4, n_words, 256), F32),
            V((2, 2, 4, WS, 256), BF16),
            V((2, 2, 4, WS, 256), BF16),
            V((4, 4, WS, 256), BF16),
            D((4,)),
            D((2,)),
            D((2, 7)),
            D((2, 7)),
            D((2, 8)),
            D((2, 4, 4)),
            D((2, 4, 4)),
            D((2, 2, 4)),
            D((2, 2, 4)),
            D((2, 4, 4)),
            D((2, 4, 4)),
            D((2, 4, 4)),
        ],
        compiler_params=pltpu.CompilerParams(
            collective_id=0, has_side_effects=True, vmem_limit_bytes=40 << 20
        ),
        name="decoder_gradients",
    )(doc_topics, word_logits, log_norm.reshape(1, width), tile_doc, tile_word, word_counts)


def solution(mesh):
    placed = (
        P("doc", "topic"),
        P("vocab", "topic"),
        P("topic"),
        P(("doc", "vocab")),
        P(("doc", "vocab")),
        P(("doc", "vocab"), None, None),
    )
    return jax.shard_map(
        on_device,
        mesh=mesh,
        in_specs=placed,
        out_specs=(P("doc", ("topic", "vocab")), P("vocab", "topic")),
        check_vma=False,
    )
```

```python
import functools

import jax
import jax.numpy as jnp
from jax import lax
from jax.experimental import pallas as pl
from jax.experimental.pallas import tpu as pltpu
from jax.sharding import PartitionSpec as P

MESH = pl.DeviceIdType.MESH
F32 = jnp.float32
BF16 = jnp.bfloat16
DT = 4
WT = 4
DS = 128
WS = 64
Z_ORDER = (4, 3, 5, 2, 6, 1, 7)
Z_ARRIVE = (1, 7, 2, 6, 3, 5, 4)


def kernel(
    docs_hbm, logits_hbm, norm_hbm, tdoc_hbm, tword_hbm, counts_hbm,
    th_fin, be_fin,
    docs, logits, norm_ref, tdoc_ref, tword_ref, counts, wp,
    rate_b, c_in, z_out, z_in, rt, rt_t, rw,
    th, y_out, y_in,
    be, x_out, x_in,
    load_sem, c_sem, z_sem, g_sem, f_sem, y_send, y_recv, x_send, x_recv, a_send, a_recv,
):
    i, t, l = (lax.axis_index(a) for a in ("doc", "topic", "vocab"))
    z, c = lax.div(t, 2), lax.rem(t, 2)
    other = (i, 2 * z + 1 - c, l)

    def z_peer(d):
        return (i, lax.rem(t + 2 * d, 16), l)

    def y_peer(d):
        return (i, t, lax.rem(l + d + 8, 8))

    def x_peer(d):
        return (lax.rem(i + d + 4, 4), t, l)

    loads = [
        pltpu.make_async_copy(norm_hbm, norm_ref, load_sem.at[4]),
        pltpu.make_async_copy(logits_hbm, logits, load_sem.at[0]),
        pltpu.make_async_copy(docs_hbm.at[pl.ds(0, 256)], docs.at[pl.ds(0, 256)], load_sem.at[1]),
        pltpu.make_async_copy(docs_hbm.at[pl.ds(256, 256)], docs.at[pl.ds(256, 256)], load_sem.at[2]),
        pltpu.make_async_copy(counts_hbm, counts, load_sem.at[3]),
        pltpu.make_async_copy(tdoc_hbm, tdoc_ref, load_sem.at[5]),
        pltpu.make_async_copy(tword_hbm, tword_ref, load_sem.at[6]),
    ]
    for cp in loads:
        cp.start()

    barrier = pltpu.get_barrier_semaphore()
    partners = [other] + [z_peer(d) for d in range(1, 8)]
    partners += [y_peer(1), y_peer(-1), x_peer(1), x_peer(-1)]
    for dev in partners:
        pl.semaphore_signal(barrier, inc=1, device_id=dev, device_id_type=MESH)

    loads[0].wait()
    loads[1].wait()
    wp[...] = jnp.exp(logits[...].astype(F32) - norm_ref[...]).astype(BF16)
    for h in range(2):
        loads[2 + h].wait()
        rate = lax.dot_general(
            wp[...], docs[pl.ds(256 * h, 256), :], (((1,), (1,)), ((), ())), preferred_element_type=F32
        ).astype(BF16)
        for k in range(2):
            for w in range(WT):
                p = (2 * h + k) * WT + w
                rate_b[p % 2, p // 2] = rate[w * WS:(w + 1) * WS, k * DS:(k + 1) * DS]
    for cp in loads[4:]:
        cp.wait()

    pl.semaphore_wait(barrier, len(partners))

    swap = pltpu.make_async_remote_copy(
        rate_b.at[1 - c], c_in, c_sem.at[0], c_sem.at[1], device_id=other, device_id_type=MESH
    )
    swap.start()
    slot = jnp.int32(0)
    for s in range(tdoc_ref.shape[0]):
        slot = jnp.where(tdoc_ref[s] * WT + tword_ref[s] == t, s, slot)
    count = counts[slot].astype(F32)
    swap.wait()
    z_out[...] = (rate_b[c].astype(F32) + c_in[...].astype(F32)).astype(BF16)

    scatter = []
    for d in Z_ORDER:
        cp = pltpu.make_async_remote_copy(
            z_out.at[lax.rem(z + d, 8)], z_in.at[d - 1], z_sem.at[0, d - 1], z_sem.at[1, d - 1],
            device_id=z_peer(d), device_id_type=MESH,
        )
        cp.start()
        scatter.append((d, cp))
    total = z_out[z].astype(F32)
    waits = dict(scatter)
    for d in (7, 1, 6, 2, 5, 3, 4):
        waits[d].wait_recv()
        total += z_in[d - 1].astype(F32)
    rt[t] = (-count / (WS * total)).astype(BF16)

    def fwd(src_t):
        return pltpu.make_async_remote_copy(
            rt.at[src_t], rt.at[src_t], f_sem.at[0, lax.div(src_t, 2)], f_sem.at[1, lax.div(src_t, 2)],
            device_id=other, device_id_type=MESH,
        )

    gather = {}
    for d in Z_ORDER:
        cp = pltpu.make_async_remote_copy(
            rt.at[t], rt.at[t], g_sem.at[0, d - 1], g_sem.at[1, d - 1],
            device_id=z_peer(d), device_id_type=MESH,
        )
        cp.start()
        gather[d] = cp
    mine = fwd(t)
    mine.start()
    passed = [mine]
    for d in Z_ARRIVE:
        src_t = lax.rem(t - 2 * d + 16, 16)
        pltpu.make_async_remote_copy(
            rt.at[src_t], rt.at[src_t], g_sem.at[0, d - 1], g_sem.at[1, d - 1],
            device_id=z_peer(d), device_id_type=MESH,
        ).wait_recv()
        cp = fwd(src_t)
        cp.start()
        passed.append(cp)
    for q in range(8):
        src_t = 2 * q + 1 - c
        pltpu.make_async_remote_copy(
            rt.at[src_t], rt.at[src_t], f_sem.at[0, q], f_sem.at[1, q], device_id=other, device_id_type=MESH
        ).wait_recv()

    for s in range(DT):
        tile = rt[pl.ds(s * WT, WT)].reshape(WT * WS, DS)
        rw[:, pl.ds(s * DS, DS)] = tile
        rt_t[pl.ds(s * DS, DS), :] = tile.T

    def theta(q):
        cols = pl.ds(pl.multiple_of(q * 128, 128), 128)
        th[q] = lax.dot_general(
            rt_t[...], wp[:, cols], (((1,), (0,)), ((), ())), preferred_element_type=F32
        )

    def beta(e):
        cols = pl.ds(pl.multiple_of(e * 256, 256), 256)
        be[e] = lax.dot_general(
            rw[...], docs[:, cols], (((1,), (0,)), ((), ())), preferred_element_type=F32
        )

    y_early = ((0, 1), (2, 3))
    y_order = ((2, 3, 0, 1), (0, 1, 2, 3))
    pending = []

    def y_copy(way, step, s):
        return pltpu.make_async_remote_copy(
            y_out.at[way, step, s], y_in.at[way, step, s], y_send.at[way, step, s], y_recv.at[way, step, s],
            device_id=y_peer(1 - 2 * way), device_id_type=MESH,
        )

    def y_go(way, step, s):
        sign = 1 - 2 * way
        q = lax.rem(l + sign * (4 - step) + 8, 8)
        v = th[q, pl.ds(s * DS, DS), :]
        if step > 1 or (step == 1 and s in y_early[way]):
            y_copy(way, step - 1, s).wait_recv()
            v = v + y_in[way, step - 1, s].astype(F32)
        y_out[way, step, s] = v.astype(BF16)
        cp = y_copy(way, step, s)
        cp.start()
        pending.append(cp)

    def x_copy(way, step, u):
        return pltpu.make_async_remote_copy(
            x_out.at[way, step, u], x_in.at[way, step, u], x_send.at[way, step, u], x_recv.at[way, step, u],
            device_id=x_peer(1 - 2 * way), device_id_type=MESH,
        )

    def x_go(way, step, u):
        sign = 1 - 2 * way
        e = lax.rem(i + sign * (2 - step) + 4, 4)
        v = be[e, pl.ds(u * WS, WS), :]
        if step == 1 and u in y_early[way]:
            x_copy(way, 0, u).wait_recv()
            v = v + x_in[way, 0, u].astype(F32)
        x_out[way, step, u] = v.astype(BF16)
        cp = x_copy(way, step, u)
        cp.start()
        pending.append(cp)

    def a_copy(way, e, u):
        hop = lax.rem(i - e + 4, 4)
        return pltpu.make_async_remote_copy(
            be_fin.at[e, pl.ds(u * WS, WS)], be_fin.at[e, pl.ds(u * WS, WS)], a_send.at[way, e, u], a_recv.at[way, e, u],
            device_id=x_peer(1 - 2 * way), device_id_type=MESH,
        )

    theta(lax.rem(l + 4, 8))
    for way in range(2):
        for s in y_early[way]:
            y_go(way, 0, s)
    beta(lax.rem(i + 2, 4))
    for way in range(2):
        for u in y_early[way]:
            x_go(way, 0, u)
    theta(lax.rem(l + 3, 8))
    theta(lax.rem(l + 5, 8))
    for way in range(2):
        for s in y_early[1 - way]:
            y_go(way, 1, s)
    beta(lax.rem(i + 1, 4))
    beta(lax.rem(i + 3, 4))
    for way in range(2):
        for u in y_early[1 - way]:
            x_go(way, 1, u)
    theta(lax.rem(l + 2, 8))
    theta(lax.rem(l + 6, 8))
    beta(i)
    theta(lax.rem(l + 1, 8))
    theta(lax.rem(l + 7, 8))
    theta(l)
    for k in range(2):
        for way in range(2):
            y_go(way, 1, y_early[way][k])
        for way in range(2):
            x_go(way, 1, y_early[way][k])
    for k in range(4):
        for way in range(2):
            y_go(way, 2, y_order[way][k])

    for u in range(4):
        for way in range(2):
            x_copy(way, 1, u).wait_recv()
        v = be[i, pl.ds(u * WS, WS), :] + x_in[0, 1, u].astype(F32) + x_in[1, 1, u].astype(F32)
        w = wp[pl.ds(u * WS, WS), pl.ds(pl.multiple_of(i * 256, 256), 256)].astype(F32)
        be_fin[i, pl.ds(u * WS, WS), :] = (v * w).astype(BF16)
        for way in range(2):
            cp = a_copy(way, i, u)
            cp.start()
            pending.append(cp)
    for k in range(4):
        for way in range(2):
            y_go(way, 3, y_order[way][k])
    for u in range(4):
        for way in range(2):
            e = lax.rem(i - (1 - 2 * way) + 4, 4)
            a_copy(way, e, u).wait_recv()
            if u in y_early[way]:
                cp = a_copy(way, e, u)
                cp.start()
                pending.append(cp)
    for k in range(4):
        s = k
        for way in range(2):
            y_copy(way, 3, s).wait_recv()
        th_fin[pl.ds(s * DS, DS), :] = (
            th[l, pl.ds(s * DS, DS), :] + y_in[0, 3, s].astype(F32) + y_in[1, 3, s].astype(F32)
        )
    e = lax.rem(i + 2, 4)
    for way in range(2):
        for u in y_early[way]:
            a_copy(way, e, u).wait_recv()

    for cp in [waits[d] for d in Z_ORDER] + [gather[d] for d in Z_ORDER] + passed + pending:
        cp.wait_send()


def finish(th_ref, be_ref, theta_hbm, beta_hbm, sem):
    copies = [pltpu.make_async_copy(th_ref, theta_hbm, sem.at[4])]
    for e in range(4):
        copies.append(pltpu.make_async_copy(be_ref.at[e], beta_hbm.at[:, pl.ds(e * 256, 256)], sem.at[e]))
    for cp in copies:
        cp.start()
    for cp in copies:
        cp.wait()


def on_device(doc_topics, word_logits, log_norm, tile_doc, tile_word, word_counts):
    n_docs, width = doc_topics.shape
    n_words = word_logits.shape[0]
    slots = tile_doc.shape[0]
    hbm = pl.BlockSpec(memory_space=pltpu.HBM)
    vmem = pl.BlockSpec(memory_space=pltpu.VMEM)
    V, D = pltpu.VMEM, pltpu.SemaphoreType.DMA
    operands = (doc_topics, word_logits, log_norm.reshape(1, width), tile_doc, tile_word, word_counts)
    theta, beta = pl.pallas_call(
        kernel,
        out_shape=(
            jax.ShapeDtypeStruct((n_docs, 128), F32),
            jax.ShapeDtypeStruct((4, n_words, 256), BF16),
        ),
        in_specs=[hbm] * 6,
        out_specs=(vmem, vmem),
        scratch_shapes=[
            V((n_docs, width), BF16),
            V((n_words, width), BF16),
            V((1, width), F32),
            pltpu.SMEM((slots,), jnp.int32),
            pltpu.SMEM((slots,), jnp.int32),
            V(word_counts.shape, jnp.int32),
            V((n_words, width), BF16),
            V((2, 8, WS, DS), BF16),
            V((8, WS, DS), BF16),
            V((8, WS, DS), BF16),
            V((7, WS, DS), BF16),
            V((16, WS, DS), BF16),
            V((n_docs, n_words), BF16),
            V((n_words, n_docs), BF16),
            V((8, n_docs, 128), F32),
            V((2, 4, 4, DS, 128), BF16),
            V((2, 4, 4, DS, 128), BF16),
            V((4, n_words, 256), F32),
            V((2, 2, 4, WS, 256), BF16),
            V((2, 2, 4, WS, 256), BF16),
            D((7,)),
            D((2,)),
            D((2, 7)),
            D((2, 7)),
            D((2, 8)),
            D((2, 4, 4)),
            D((2, 4, 4)),
            D((2, 2, 4)),
            D((2, 2, 4)),
            D((2, 4, 4)),
            D((2, 4, 4)),
        ],
        compiler_params=pltpu.CompilerParams(
            collective_id=0, has_side_effects=True, vmem_limit_bytes=40 << 20
        ),
        name="decoder_gradients",
    )(*(pltpu.with_memory_space_constraint(x, pltpu.HBM) for x in operands))
    return pl.pallas_call(
        finish,
        out_shape=(
            jax.ShapeDtypeStruct((n_docs, 128), F32),
            jax.ShapeDtypeStruct((n_words, width), BF16),
        ),
        in_specs=[pl.BlockSpec(memory_space=pl.ANY)] * 2,
        out_specs=(hbm, hbm),
        scratch_shapes=[D((5,))],
        name="write_out",
    )(*(pltpu.with_memory_space_constraint(x, pltpu.VMEM) for x in (theta, beta)))


def solution(mesh):
    placed = (
        P("doc", "topic"),
        P("vocab", "topic"),
        P("topic"),
        P(("doc", "vocab")),
        P(("doc", "vocab")),
        P(("doc", "vocab"), None, None),
    )
    return jax.shard_map(
        on_device,
        mesh=mesh,
        in_specs=placed,
        out_specs=(P("doc", ("topic", "vocab")), P("vocab", "topic")),
        check_vma=False,
    )
```

```python
import jax
import jax.numpy as jnp
from jax import lax
from jax.experimental import pallas as pl
from jax.experimental.pallas import tpu as pltpu
from jax.sharding import PartitionSpec as P

MESH = pl.DeviceIdType.MESH
F32 = jnp.float32
BF16 = jnp.bfloat16
DT = 4
WT = 4
DS = 128
WS = 64
Z_ORDER = (4, 3, 5, 2, 6, 1, 7)
Z_ARRIVE = (1, 7, 2, 6, 3, 5, 4)


def kernel(
    docs_hbm, logits_hbm, norm_hbm, tdoc_hbm, tword_hbm, counts_hbm,
    th_fin, be_fin,
    docs, logits, norm_ref, tdoc_ref, tword_ref, counts, wp,
    rate_b, c_in, z_out, z_in, rt, rt_t, rw,
    th, y_out, y_in,
    be, x_out, x_in,
    load_sem, c_sem, send_sem, z_recv, g_recv, f_recv, y_recv, x_recv, a_recv,
):
    i, t, l = (lax.axis_index(a) for a in ("doc", "topic", "vocab"))
    z, c = lax.div(t, 2), lax.rem(t, 2)
    loads = [
        pltpu.make_async_copy(norm_hbm, norm_ref, load_sem.at[0]),
        pltpu.make_async_copy(logits_hbm, logits, load_sem.at[1]),
        pltpu.make_async_copy(docs_hbm.at[pl.ds(0, 256)], docs.at[pl.ds(0, 256)], load_sem.at[2]),
        pltpu.make_async_copy(docs_hbm.at[pl.ds(256, 256)], docs.at[pl.ds(256, 256)], load_sem.at[3]),
        pltpu.make_async_copy(counts_hbm, counts, load_sem.at[4]),
        pltpu.make_async_copy(tdoc_hbm, tdoc_ref, load_sem.at[5]),
        pltpu.make_async_copy(tword_hbm, tword_ref, load_sem.at[6]),
    ]
    for cp in loads:
        cp.start()

    other = (i, 2 * z + 1 - c, l)
    z_at = [lax.rem(z + d, 8) for d in range(8)]
    z_to = [(i, 2 * z_at[d] + c, l) for d in range(8)]
    y_at = [lax.rem(l + d, 8) for d in range(8)]
    x_at = [lax.rem(i + d, 4) for d in range(4)]
    y_to = [(i, t, y_at[1]), (i, t, y_at[7])]
    x_to = [(x_at[1], t, l), (x_at[3], t, l)]

    barrier = pltpu.get_barrier_semaphore()
    partners = z_to[1:] + [other] + y_to + x_to
    for dev in partners:
        pl.semaphore_signal(barrier, inc=1, device_id=dev, device_id_type=MESH)

    def remote(src, dst, send, recv, dev):
        return pltpu.make_async_remote_copy(src, dst, send, recv, device_id=dev, device_id_type=MESH)

    loads[0].wait()
    loads[1].wait()
    wp[...] = jnp.exp(logits[...].astype(F32) - norm_ref[...]).astype(BF16)
    for h in range(2):
        loads[2 + h].wait()
        rate = lax.dot_general(
            wp[...], docs[pl.ds(256 * h, 256), :], (((1,), (1,)), ((), ())), preferred_element_type=F32
        ).astype(BF16)
        for k in range(2):
            for w in range(WT):
                p = (2 * h + k) * WT + w
                rate_b[p % 2, p // 2] = rate[w * WS:(w + 1) * WS, k * DS:(k + 1) * DS]
    for cp in loads[4:]:
        cp.wait()

    pl.semaphore_wait(barrier, len(partners))

    swap = remote(rate_b.at[1 - c], c_in, c_sem.at[0], c_sem.at[1], other)
    swap.start()
    slot = jnp.int32(0)
    for s in range(tdoc_ref.shape[0]):
        slot = jnp.where(tdoc_ref[s] * WT + tword_ref[s] == t, s, slot)
    count = counts[slot].astype(F32)
    swap.wait_recv()
    z_out[...] = (rate_b[c].astype(F32) + c_in[...].astype(F32)).astype(BF16)

    for d in Z_ORDER:
        remote(z_out.at[z_at[d]], z_in.at[d - 1], send_sem.at[0], z_recv.at[0], z_to[d]).start()
    total = z_out[z].astype(F32)
    remote(z_in, z_in, send_sem.at[0], z_recv.at[0], other).wait_recv()
    for d in range(1, 8):
        total += z_in[d - 1].astype(F32)
    rt[c, z] = (-count / (WS * total)).astype(BF16)

    mine = rt.at[c, z]
    for d in Z_ORDER:
        remote(mine, mine, send_sem.at[1], g_recv.at[d - 1], z_to[d]).start()
    remote(mine, mine, send_sem.at[2], f_recv.at[0], other).start()
    for d in Z_ARRIVE:
        tile = rt.at[c, z_at[8 - d]]
        remote(tile, tile, send_sem.at[1], g_recv.at[d - 1], other).wait_recv()
        remote(tile, tile, send_sem.at[2], f_recv.at[0], other).start()
    remote(rt.at[1 - c], rt.at[1 - c], send_sem.at[2], f_recv.at[0], other).wait_recv()

    for s in range(DT):
        tiles = [rt[w % 2, 2 * s + w // 2] for w in range(WT)]
        tile = jnp.concatenate(tiles, axis=0)
        rw[:, pl.ds(s * DS, DS)] = tile
        rt_t[pl.ds(s * DS, DS), :] = tile.T

    def theta(d):
        cols = pl.ds(pl.multiple_of(y_at[d] * 128, 128), 128)
        th[y_at[d]] = lax.dot_general(
            rt_t[...], wp[:, cols], (((1,), (0,)), ((), ())), preferred_element_type=F32
        )

    def beta(d):
        cols = pl.ds(pl.multiple_of(x_at[d] * 256, 256), 256)
        be[x_at[d]] = lax.dot_general(
            rw[...], docs[:, cols], (((1,), (0,)), ((), ())), preferred_element_type=F32
        )

    HD, HW = 2 * DS, 2 * WS

    def y_copy(way, step, early):
        k = 7 * way + 2 * step - (0 if early else 1)
        return remote(y_out.at[k], y_in.at[k], send_sem.at[3], y_recv.at[k], y_to[way]), k

    def y_go(step, early):
        for way in range(2):
            h = way if early else 1 - way
            d = 4 - step if way == 0 else 4 + step
            v = th[y_at[d], pl.ds(h * HD, HD), :]
            if step > 1 or (step == 1 and early):
                cp, k = y_copy(way, step - 1, early)
                cp.wait_recv()
                v = v + y_in[k].astype(F32)
            cp, k = y_copy(way, step, early)
            y_out[k] = v.astype(BF16)
            cp.start()

    def x_copy(way, step, early):
        k = 3 * way + 2 * step - (0 if early else 1)
        return remote(x_out.at[k], x_in.at[k], send_sem.at[4], x_recv.at[k], x_to[way]), k

    def x_go(step, early):
        for way in range(2):
            h = way if early else 1 - way
            d = 2 - step if way == 0 else 2 + step
            v = be[x_at[d], pl.ds(h * HW, HW), :]
            if step == 1 and early:
                cp, k = x_copy(way, 0, True)
                cp.wait_recv()
                v = v + x_in[k].astype(F32)
            cp, k = x_copy(way, step, early)
            x_out[k] = v.astype(BF16)
            cp.start()

    def a_copy(way, kind, e):
        h = 1 - way if kind == 1 else way
        rows = be_fin.at[e, pl.ds(h * HW, HW)]
        return remote(rows, rows, send_sem.at[5], a_recv.at[3 * way + kind], x_to[way])

    def beta_whole():
        for h in range(2):
            cp, early = x_copy(h, 1, True)
            cp.wait_recv()
            cp, late = x_copy(1 - h, 1, False)
            cp.wait_recv()
            rows = pl.ds(h * HW, HW)
            v = be[i, rows, :] + x_in[early].astype(F32) + x_in[late].astype(F32)
            w = wp[rows, pl.ds(pl.multiple_of(i * 256, 256), 256)].astype(F32)
            be_fin[i, rows, :] = (v * w).astype(BF16)
            a_copy(h, 0, i).start()
        for way in range(2):
            a_copy(way, 1, i).start()

    def from_way(way):
        return x_at[3] if way == 0 else x_at[1]

    theta(4)
    y_go(0, True)
    beta(2)
    x_go(0, True)
    theta(3)
    theta(5)
    y_go(1, False)
    beta(1)
    beta(3)
    x_go(1, False)
    theta(2)
    theta(6)
    beta(0)
    y_go(1, True)
    x_go(1, True)
    theta(1)
    theta(7)
    theta(0)
    y_go(2, False)
    y_go(2, True)
    beta_whole()
    y_go(3, False)
    y_go(3, True)
    for way in range(2):
        a_copy(way, 0, from_way(way)).wait_recv()
        a_copy(way, 2, from_way(way)).start()
    for h in range(2):
        cp, late = y_copy(1 - h, 3, False)
        cp.wait_recv()
        cp, early = y_copy(h, 3, True)
        cp.wait_recv()
        rows = pl.ds(h * HD, HD)
        th_fin[rows, :] = th[l, rows, :] + y_in[early].astype(F32) + y_in[late].astype(F32)
    for way in range(2):
        a_copy(way, 1, from_way(way)).wait_recv()
    for way in range(2):
        a_copy(way, 2, x_at[2]).wait_recv()

    remote(rate_b.at[1 - c], c_in, c_sem.at[0], c_sem.at[1], other).wait_send()
    remote(z_in, z_in, send_sem.at[0], z_recv.at[0], other).wait_send()
    remote(z_in, z_in, send_sem.at[1], z_recv.at[0], other).wait_send()
    remote(z_out, z_out, send_sem.at[2], z_recv.at[0], other).wait_send()
    remote(y_out, y_in, send_sem.at[3], z_recv.at[0], other).wait_send()
    remote(x_out, x_in, send_sem.at[4], z_recv.at[0], other).wait_send()
    remote(x_out, x_in, send_sem.at[5], z_recv.at[0], other).wait_send()


def finish(th_ref, be_ref, theta_hbm, beta_hbm, sem):
    copies = [pltpu.make_async_copy(th_ref, theta_hbm, sem.at[4])]
    for e in range(4):
        copies.append(pltpu.make_async_copy(be_ref.at[e], beta_hbm.at[:, pl.ds(e * 256, 256)], sem.at[e]))
    for cp in copies:
        cp.start()
    for cp in copies:
        cp.wait()


def on_device(doc_topics, word_logits, log_norm, tile_doc, tile_word, word_counts):
    n_docs, width = doc_topics.shape
    n_words = word_logits.shape[0]
    slots = tile_doc.shape[0]
    hbm = pl.BlockSpec(memory_space=pltpu.HBM)
    vmem = pl.BlockSpec(memory_space=pltpu.VMEM)
    V, D = pltpu.VMEM, pltpu.SemaphoreType.DMA
    operands = (doc_topics, word_logits, log_norm.reshape(1, width), tile_doc, tile_word, word_counts)
    theta, beta = pl.pallas_call(
        kernel,
        out_shape=(
            jax.ShapeDtypeStruct((n_docs, 128), F32),
            jax.ShapeDtypeStruct((4, n_words, 256), BF16),
        ),
        in_specs=[hbm] * 6,
        out_specs=(vmem, vmem),
        scratch_shapes=[
            V((n_docs, width), BF16),
            V((n_words, width), BF16),
            V((1, width), F32),
            pltpu.SMEM((slots,), jnp.int32),
            pltpu.SMEM((slots,), jnp.int32),
            V(word_counts.shape, jnp.int32),
            V((n_words, width), BF16),
            V((2, 8, WS, DS), BF16),
            V((8, WS, DS), BF16),
            V((8, WS, DS), BF16),
            V((7, WS, DS), BF16),
            V((2, 8, WS, DS), BF16),
            V((n_docs, n_words), BF16),
            V((n_words, n_docs), BF16),
            V((8, n_docs, 128), F32),
            V((14, 2 * DS, 128), BF16),
            V((14, 2 * DS, 128), BF16),
            V((4, n_words, 256), F32),
            V((6, 2 * WS, 256), BF16),
            V((6, 2 * WS, 256), BF16),
            D((7,)),
            D((2,)),
            D((6,)),
            D((1,)),
            D((7,)),
            D((1,)),
            D((14,)),
            D((6,)),
            D((6,)),
        ],
        compiler_params=pltpu.CompilerParams(
            collective_id=0, has_side_effects=True, vmem_limit_bytes=40 << 20
        ),
        name="decoder_gradients",
    )(*(pltpu.with_memory_space_constraint(x, pltpu.HBM) for x in operands))
    return pl.pallas_call(
        finish,
        out_shape=(
            jax.ShapeDtypeStruct((n_docs, 128), F32),
            jax.ShapeDtypeStruct((n_words, width), BF16),
        ),
        in_specs=[pl.BlockSpec(memory_space=pl.ANY)] * 2,
        out_specs=(hbm, hbm),
        scratch_shapes=[D((5,))],
        name="write_out",
    )(*(pltpu.with_memory_space_constraint(x, pltpu.VMEM) for x in (theta, beta)))


def solution(mesh):
    placed = (
        P("doc", "topic"),
        P("vocab", "topic"),
        P("topic"),
        P(("doc", "vocab")),
        P(("doc", "vocab")),
        P(("doc", "vocab"), None, None),
    )
    return jax.shard_map(
        on_device,
        mesh=mesh,
        in_specs=placed,
        out_specs=(P("doc", ("topic", "vocab")), P("vocab", "topic")),
        check_vma=False,
    )
```

```python
import jax
import jax.numpy as jnp
from jax import lax
from jax.experimental import pallas as pl
from jax.experimental.pallas import tpu as pltpu
from jax.sharding import PartitionSpec as P

MESH = pl.DeviceIdType.MESH
F32 = jnp.float32
BF16 = jnp.bfloat16
DT = 4
WT = 4
DS = 128
WS = 64
Z_ORDER = (4, 3, 5, 2, 6, 1, 7)
Z_ARRIVE = (1, 7, 2, 6, 3, 5, 4)


def kernel(
    docs_hbm, logits_hbm, norm_hbm, tdoc_hbm, tword_hbm, counts_hbm,
    th_fin, be_fin,
    docs, logits, norm_ref, tdoc_ref, tword_ref, counts, wp,
    rate_b, c_in, z_out, z_in, rt, rt_t, rw,
    th, y_out, y_in,
    be, x_out, x_in,
    load_sem, c_sem, send_sem, z_recv, g_recv, f_recv, y_recv, x_recv, a_recv, ready, column,
):
    i, t, l = (lax.axis_index(a) for a in ("doc", "topic", "vocab"))
    z, c = lax.div(t, 2), lax.rem(t, 2)
    loads = [
        pltpu.make_async_copy(norm_hbm, norm_ref, load_sem.at[0]),
        pltpu.make_async_copy(logits_hbm, logits, load_sem.at[1]),
        pltpu.make_async_copy(docs_hbm.at[pl.ds(0, 256)], docs.at[pl.ds(0, 256)], load_sem.at[2]),
        pltpu.make_async_copy(docs_hbm.at[pl.ds(256, 256)], docs.at[pl.ds(256, 256)], load_sem.at[3]),
        pltpu.make_async_copy(counts_hbm, counts, load_sem.at[4]),
        pltpu.make_async_copy(tdoc_hbm, tdoc_ref, load_sem.at[5]),
        pltpu.make_async_copy(tword_hbm, tword_ref, load_sem.at[6]),
    ]
    for cp in loads[:4]:
        cp.start()

    other = (i, 2 * z + 1 - c, l)
    z_dev = [(i, 2 * k + c, l) for k in range(8)]
    z_at = [lax.rem(z + d, 8) for d in range(8)]
    z_to = [(i, 2 * z_at[d] + c, l) for d in range(8)]
    y_at = [lax.rem(l + d, 8) for d in range(8)]
    x_at = [lax.rem(i + d, 4) for d in range(4)]
    y_to = [(i, t, y_at[1]), (i, t, y_at[7])]
    x_to = [(x_at[1], t, l), (x_at[3], t, l)]

    def signal(sem, dev):
        pl.semaphore_signal(sem, inc=1, device_id=dev, device_id_type=MESH)

    barrier = pltpu.get_barrier_semaphore()
    signal(barrier, other)
    for k in range(1, 8):
        @pl.when(z < k)
        def _():
            signal(barrier, z_dev[k])

    @pl.when(z == 0)
    def _():
        for dev in y_to + x_to:
            signal(barrier, dev)
        pl.semaphore_wait(barrier, 5)

    @pl.when(z > 0)
    def _():
        pl.semaphore_wait(barrier, z + 1)

    for k in (3, 2, 4, 1, 5, 0, 6):
        @pl.when(z > k)
        def _():
            signal(ready.at[z], z_dev[k])

    def remote(src, dst, send, recv, dev):
        return pltpu.make_async_remote_copy(src, dst, send, recv, device_id=dev, device_id_type=MESH)

    def swap(h):
        part = pl.ds(4 * h, 4)
        return remote(rate_b.at[1 - c, part], c_in.at[part], c_sem.at[2], c_sem.at[h], other)

    loads[0].wait()
    loads[1].wait()
    wp[...] = jnp.exp(logits[...].astype(F32) - norm_ref[...]).astype(BF16)
    for h in range(2):
        loads[2 + h].wait()
        rate = lax.dot_general(
            wp[...], docs[pl.ds(256 * h, 256), :], (((1,), (1,)), ((), ())), preferred_element_type=F32
        ).astype(BF16)
        for k in range(2):
            for w in range(WT):
                p = (2 * h + k) * WT + w
                rate_b[p % 2, p // 2] = rate[w * WS:(w + 1) * WS, k * DS:(k + 1) * DS]
        swap(h).start()
    for cp in loads[4:]:
        cp.start()

    for h in range(2):
        part = pl.ds(4 * h, 4)
        swap(h).wait_recv()
        z_out[part] = (rate_b[c, part].astype(F32) + c_in[part].astype(F32)).astype(BF16)
        for k in (3, 2, 1, 0) if h == 0 else (4, 5, 6, 7):
            @pl.when(z < k)
            def _():
                pl.semaphore_wait(ready.at[k], 1)

            @pl.when(z != k)
            def _():
                remote(z_out.at[k], z_in.at[z], send_sem.at[0], z_recv.at[0], z_dev[k]).start()
    z_in[z] = z_out[z]

    @pl.when(z == 0)
    def _():
        for dev in y_to + x_to:
            signal(column.at[0], dev)

    for cp in loads[4:]:
        cp.wait()
    slot = jnp.int32(0)
    for s in range(tdoc_ref.shape[0]):
        slot = jnp.where(tdoc_ref[s] * WT + tword_ref[s] == t, s, slot)
    count = counts[slot].astype(F32)
    seven = z_in.at[pl.ds(0, 7)]
    remote(seven, seven, send_sem.at[0], z_recv.at[0], other).wait_recv()
    total = z_in[0].astype(F32)
    for k in range(1, 8):
        total += z_in[k].astype(F32)
    rt[c, z] = (-count / (WS * total)).astype(BF16)

    mine = rt.at[c, z]
    for d in Z_ORDER:
        remote(mine, mine, send_sem.at[1], g_recv.at[d - 1], z_to[d]).start()
    remote(mine, mine, send_sem.at[2], f_recv.at[0], other).start()

    @pl.when(z == 0)
    def _():
        pl.semaphore_wait(column.at[0], 4)
        for k in range(1, 8):
            signal(column.at[1], z_dev[k])

    for d in Z_ARRIVE:
        tile = rt.at[c, z_at[8 - d]]
        remote(tile, tile, send_sem.at[1], g_recv.at[d - 1], other).wait_recv()
        remote(tile, tile, send_sem.at[2], f_recv.at[0], other).start()
    remote(rt.at[1 - c], rt.at[1 - c], send_sem.at[2], f_recv.at[0], other).wait_recv()

    @pl.when(z > 0)
    def _():
        pl.semaphore_wait(column.at[1], 1)

    for s in range(DT):
        tiles = [rt[w % 2, 2 * s + w // 2] for w in range(WT)]
        tile = jnp.concatenate(tiles, axis=0)
        rw[:, pl.ds(s * DS, DS)] = tile
        rt_t[pl.ds(s * DS, DS), :] = tile.T

    def theta(d):
        cols = pl.ds(pl.multiple_of(y_at[d] * 128, 128), 128)
        th[y_at[d]] = lax.dot_general(
            rt_t[...], wp[:, cols], (((1,), (0,)), ((), ())), preferred_element_type=F32
        )

    def beta(d):
        cols = pl.ds(pl.multiple_of(x_at[d] * 256, 256), 256)
        be[x_at[d]] = lax.dot_general(
            rw[...], docs[:, cols], (((1,), (0,)), ((), ())), preferred_element_type=F32
        )

    HD, HW = 2 * DS, 2 * WS

    def y_copy(way, step, early):
        k = 7 * way + 2 * step - (0 if early else 1)
        return remote(y_out.at[k], y_in.at[k], send_sem.at[3], y_recv.at[k], y_to[way]), k

    def y_go(step, early):
        for way in range(2):
            h = way if early else 1 - way
            d = 4 - step if way == 0 else 4 + step
            v = th[y_at[d], pl.ds(h * HD, HD), :]
            if step > 1 or (step == 1 and early):
                cp, k = y_copy(way, step - 1, early)
                cp.wait_recv()
                v = v + y_in[k].astype(F32)
            cp, k = y_copy(way, step, early)
            y_out[k] = v.astype(BF16)
            cp.start()

    def x_copy(way, step, early):
        k = 3 * way + 2 * step - (0 if early else 1)
        return remote(x_out.at[k], x_in.at[k], send_sem.at[4], x_recv.at[k], x_to[way]), k

    def x_go(step, early):
        for way in range(2):
            h = way if early else 1 - way
            d = 2 - step if way == 0 else 2 + step
            v = be[x_at[d], pl.ds(h * HW, HW), :]
            if step == 1 and early:
                cp, k = x_copy(way, 0, True)
                cp.wait_recv()
                v = v + x_in[k].astype(F32)
            cp, k = x_copy(way, step, early)
            x_out[k] = v.astype(BF16)
            cp.start()

    def a_copy(way, kind, e):
        h = 1 - way if kind == 1 else way
        rows = be_fin.at[e, pl.ds(h * HW, HW)]
        return remote(rows, rows, send_sem.at[5], a_recv.at[3 * way + kind], x_to[way])

    def beta_whole():
        for h in range(2):
            cp, early = x_copy(h, 1, True)
            cp.wait_recv()
            cp, late = x_copy(1 - h, 1, False)
            cp.wait_recv()
            rows = pl.ds(h * HW, HW)
            v = be[i, rows, :] + x_in[early].astype(F32) + x_in[late].astype(F32)
            w = wp[rows, pl.ds(pl.multiple_of(i * 256, 256), 256)].astype(F32)
            be_fin[i, rows, :] = (v * w).astype(BF16)
            a_copy(h, 0, i).start()
        for way in range(2):
            a_copy(way, 1, i).start()

    def from_way(way):
        return x_at[3] if way == 0 else x_at[1]

    theta(4)
    y_go(0, True)
    beta(2)
    x_go(0, True)
    theta(3)
    theta(5)
    y_go(1, False)
    beta(1)
    beta(3)
    x_go(1, False)
    theta(2)
    theta(6)
    beta(0)
    y_go(1, True)
    x_go(1, True)
    theta(1)
    theta(7)
    theta(0)
    y_go(2, False)
    y_go(2, True)
    beta_whole()
    y_go(3, False)
    y_go(3, True)
    for way in range(2):
        a_copy(way, 0, from_way(way)).wait_recv()
        a_copy(way, 2, from_way(way)).start()
    for h in range(2):
        cp, late = y_copy(1 - h, 3, False)
        cp.wait_recv()
        cp, early = y_copy(h, 3, True)
        cp.wait_recv()
        rows = pl.ds(h * HD, HD)
        th_fin[rows, :] = th[l, rows, :] + y_in[early].astype(F32) + y_in[late].astype(F32)
    for way in range(2):
        a_copy(way, 1, from_way(way)).wait_recv()
    for way in range(2):
        a_copy(way, 2, x_at[2]).wait_recv()

    remote(c_in, c_in, c_sem.at[2], c_sem.at[0], other).wait_send()
    remote(seven, seven, send_sem.at[0], z_recv.at[0], other).wait_send()
    remote(seven, seven, send_sem.at[1], z_recv.at[0], other).wait_send()
    remote(z_out, z_out, send_sem.at[2], z_recv.at[0], other).wait_send()
    remote(y_out, y_in, send_sem.at[3], z_recv.at[0], other).wait_send()
    remote(x_out, x_in, send_sem.at[4], z_recv.at[0], other).wait_send()
    remote(x_out, x_in, send_sem.at[5], z_recv.at[0], other).wait_send()


def finish(th_ref, be_ref, theta_hbm, beta_hbm, sem):
    copies = [pltpu.make_async_copy(th_ref, theta_hbm, sem.at[4])]
    for e in range(4):
        copies.append(pltpu.make_async_copy(be_ref.at[e], beta_hbm.at[:, pl.ds(e * 256, 256)], sem.at[e]))
    for cp in copies:
        cp.start()
    for cp in copies:
        cp.wait()


def on_device(doc_topics, word_logits, log_norm, tile_doc, tile_word, word_counts):
    n_docs, width = doc_topics.shape
    n_words = word_logits.shape[0]
    slots = tile_doc.shape[0]
    hbm = pl.BlockSpec(memory_space=pltpu.HBM)
    vmem = pl.BlockSpec(memory_space=pltpu.VMEM)
    V, D = pltpu.VMEM, pltpu.SemaphoreType.DMA
    operands = (doc_topics, word_logits, log_norm.reshape(1, width), tile_doc, tile_word, word_counts)
    theta, beta = pl.pallas_call(
        kernel,
        out_shape=(
            jax.ShapeDtypeStruct((n_docs, 128), F32),
            jax.ShapeDtypeStruct((4, n_words, 256), BF16),
        ),
        in_specs=[hbm] * 6,
        out_specs=(vmem, vmem),
        scratch_shapes=[
            V((n_docs, width), BF16),
            V((n_words, width), BF16),
            V((1, width), F32),
            pltpu.SMEM((slots,), jnp.int32),
            pltpu.SMEM((slots,), jnp.int32),
            V(word_counts.shape, jnp.int32),
            V((n_words, width), BF16),
            V((2, 8, WS, DS), BF16),
            V((8, WS, DS), BF16),
            V((8, WS, DS), BF16),
            V((8, WS, DS), BF16),
            V((2, 8, WS, DS), BF16),
            V((n_docs, n_words), BF16),
            V((n_words, n_docs), BF16),
            V((8, n_docs, 128), F32),
            V((14, 2 * DS, 128), BF16),
            V((14, 2 * DS, 128), BF16),
            V((4, n_words, 256), F32),
            V((6, 2 * WS, 256), BF16),
            V((6, 2 * WS, 256), BF16),
            D((7,)),
            D((3,)),
            D((6,)),
            D((1,)),
            D((7,)),
            D((1,)),
            D((14,)),
            D((6,)),
            D((6,)),
            pltpu.SemaphoreType.REGULAR((8,)),
            pltpu.SemaphoreType.REGULAR((2,)),
        ],
        compiler_params=pltpu.CompilerParams(
            collective_id=0, has_side_effects=True, vmem_limit_bytes=40 << 20
        ),
        name="decoder_gradients",
    )(*(pltpu.with_memory_space_constraint(x, pltpu.HBM) for x in operands))
    return pl.pallas_call(
        finish,
        out_shape=(
            jax.ShapeDtypeStruct((n_docs, 128), F32),
            jax.ShapeDtypeStruct((n_words, width), BF16),
        ),
        in_specs=[pl.BlockSpec(memory_space=pl.ANY)] * 2,
        out_specs=(hbm, hbm),
        scratch_shapes=[D((5,))],
        name="write_out",
    )(*(pltpu.with_memory_space_constraint(x, pltpu.VMEM) for x in (theta, beta)))


def solution(mesh):
    placed = (
        P("doc", "topic"),
        P("vocab", "topic"),
        P("topic"),
        P(("doc", "vocab")),
        P(("doc", "vocab")),
        P(("doc", "vocab"), None, None),
    )
    return jax.shard_map(
        on_device,
        mesh=mesh,
        in_specs=placed,
        out_specs=(P("doc", ("topic", "vocab")), P("vocab", "topic")),
        check_vma=False,
    )
```

```python
import jax
import jax.numpy as jnp
from jax import lax
from jax.experimental import pallas as pl
from jax.experimental.pallas import tpu as pltpu
from jax.sharding import PartitionSpec as P

MESH = pl.DeviceIdType.MESH
F32 = jnp.float32
BF16 = jnp.bfloat16
DT = 4
WT = 4
DS = 128
WS = 64
Z_ORDER = (4, 3, 5, 2, 6, 1, 7)
Z_ARRIVE = (1, 7, 2, 6, 3, 5, 4)


def kernel(
    docs_hbm, logits_hbm, norm_hbm, tdoc_hbm, tword_hbm, counts_hbm,
    th_fin, be_fin,
    docs, logits, norm_ref, tdoc_ref, tword_ref, counts, wp,
    rate_b, c_in, z_out, z_in, rt, rt_t, rw,
    th, y_out, y_in,
    be, x_out, x_in,
    load_sem, c_sem, send_sem, z_recv, g_recv, f_recv, y_recv, x_recv, a_recv, ready, column,
):
    i, t, l = (lax.axis_index(a) for a in ("doc", "topic", "vocab"))
    z, c = lax.div(t, 2), lax.rem(t, 2)
    loads = [
        pltpu.make_async_copy(norm_hbm, norm_ref, load_sem.at[0]),
        pltpu.make_async_copy(logits_hbm, logits, load_sem.at[1]),
        pltpu.make_async_copy(docs_hbm.at[pl.ds(0, 256)], docs.at[pl.ds(0, 256)], load_sem.at[2]),
        pltpu.make_async_copy(docs_hbm.at[pl.ds(256, 256)], docs.at[pl.ds(256, 256)], load_sem.at[3]),
        pltpu.make_async_copy(counts_hbm, counts, load_sem.at[4]),
        pltpu.make_async_copy(tdoc_hbm, tdoc_ref, load_sem.at[5]),
        pltpu.make_async_copy(tword_hbm, tword_ref, load_sem.at[6]),
    ]
    for cp in loads[:4]:
        cp.start()

    other = (i, 2 * z + 1 - c, l)
    z_dev = [(i, 2 * k + c, l) for k in range(8)]
    z_at = [lax.rem(z + d, 8) for d in range(8)]
    z_to = [(i, 2 * z_at[d] + c, l) for d in range(8)]
    y_at = [lax.rem(l + d, 8) for d in range(8)]
    x_at = [lax.rem(i + d, 4) for d in range(4)]
    y_to = [(i, t, y_at[1]), (i, t, y_at[7])]
    x_to = [(x_at[1], t, l), (x_at[3], t, l)]

    def signal(sem, dev):
        pl.semaphore_signal(sem, inc=1, device_id=dev, device_id_type=MESH)

    barrier = pltpu.get_barrier_semaphore()
    signal(barrier, other)
    for k in range(1, 8):
        @pl.when(z < k)
        def _():
            signal(barrier, z_dev[k])

    @pl.when(z == 0)
    def _():
        for dev in y_to + x_to:
            signal(barrier, dev)
        pl.semaphore_wait(barrier, 5)

    @pl.when(z > 0)
    def _():
        pl.semaphore_wait(barrier, z + 1)

    for k in (3, 2, 4, 1, 5, 0, 6):
        @pl.when(z > k)
        def _():
            signal(ready.at[z], z_dev[k])

    def remote(src, dst, send, recv, dev):
        return pltpu.make_async_remote_copy(src, dst, send, recv, device_id=dev, device_id_type=MESH)

    def swap(h):
        part = pl.ds(4 * h, 4)
        return remote(rate_b.at[1 - c, part], c_in.at[part], c_sem.at[2], c_sem.at[h], other)

    loads[0].wait()
    loads[1].wait()
    wp[...] = jnp.exp(logits[...].astype(F32) - norm_ref[...]).astype(BF16)
    for h in range(2):
        loads[2 + h].wait()
        rate = lax.dot_general(
            wp[...], docs[pl.ds(256 * h, 256), :], (((1,), (1,)), ((), ())), preferred_element_type=F32
        ).astype(BF16)
        for k in range(2):
            for w in range(WT):
                p = (2 * h + k) * WT + w
                rate_b[p % 2, p // 2] = rate[w * WS:(w + 1) * WS, k * DS:(k + 1) * DS]
        swap(h).start()
    for cp in loads[4:]:
        cp.start()

    for h in range(2):
        part = pl.ds(4 * h, 4)
        swap(h).wait_recv()
        z_out[part] = (rate_b[c, part].astype(F32) + c_in[part].astype(F32)).astype(BF16)
        for k in (3, 2, 1, 0) if h == 0 else (4, 5, 6, 7):
            @pl.when(z < k)
            def _():
                pl.semaphore_wait(ready.at[k], 1)

            @pl.when(z != k)
            def _():
                remote(z_out.at[k], z_in.at[z], send_sem.at[0], z_recv.at[0], z_dev[k]).start()
    z_in[z] = z_out[z]

    @pl.when(z == 0)
    def _():
        for dev in y_to + x_to:
            signal(column.at[0], dev)

    for cp in loads[4:]:
        cp.wait()
    slot = jnp.int32(0)
    for s in range(tdoc_ref.shape[0]):
        slot = jnp.where(tdoc_ref[s] * WT + tword_ref[s] == t, s, slot)
    count = counts[slot].astype(F32)
    seven = z_in.at[pl.ds(0, 7)]
    remote(seven, seven, send_sem.at[0], z_recv.at[0], other).wait_recv()
    total = z_in[0].astype(F32)
    for k in range(1, 8):
        total += z_in[k].astype(F32)
    rt[c, z] = (-count / (WS * total)).astype(BF16)

    mine = rt.at[c, z]
    for d in Z_ORDER:
        remote(mine, mine, send_sem.at[1], g_recv.at[d - 1], z_to[d]).start()
    remote(mine, mine, send_sem.at[2], f_recv.at[0], other).start()

    @pl.when(z == 0)
    def _():
        pl.semaphore_wait(column.at[0], 4)
        for k in range(1, 8):
            signal(column.at[1], z_dev[k])

    for d in Z_ARRIVE:
        tile = rt.at[c, z_at[8 - d]]
        remote(tile, tile, send_sem.at[1], g_recv.at[d - 1], other).wait_recv()
        remote(tile, tile, send_sem.at[2], f_recv.at[0], other).start()
    remote(rt.at[1 - c], rt.at[1 - c], send_sem.at[2], f_recv.at[0], other).wait_recv()

    @pl.when(z > 0)
    def _():
        pl.semaphore_wait(column.at[1], 1)

    for s in range(DT):
        tiles = [rt[w % 2, 2 * s + w // 2] for w in range(WT)]
        tile = jnp.concatenate(tiles, axis=0)
        rw[:, pl.ds(s * DS, DS)] = tile
        rt_t[pl.ds(s * DS, DS), :] = tile.T

    def theta(d):
        cols = pl.ds(pl.multiple_of(y_at[d] * 128, 128), 128)
        th[y_at[d]] = lax.dot_general(
            rt_t[...], wp[:, cols], (((1,), (0,)), ((), ())), preferred_element_type=F32
        )

    def beta(d):
        cols = pl.ds(pl.multiple_of(x_at[d] * 256, 256), 256)
        be[x_at[d]] = lax.dot_general(
            rw[...], docs[:, cols], (((1,), (0,)), ((), ())), preferred_element_type=F32
        )

    HD, HW = 2 * DS, 2 * WS

    def y_copy(way, step, early):
        k = 7 * way + 2 * step - (0 if early else 1)
        return remote(y_out.at[k], y_in.at[k], send_sem.at[3], y_recv.at[k], y_to[way]), k

    def y_go(step, early):
        for way in range(2):
            h = way if early else 1 - way
            d = 4 - step if way == 0 else 4 + step
            v = th[y_at[d], pl.ds(h * HD, HD), :]
            if step > 1 or (step == 1 and early):
                cp, k = y_copy(way, step - 1, early)
                cp.wait_recv()
                v = v + y_in[k].astype(F32)
            cp, k = y_copy(way, step, early)
            y_out[k] = v.astype(BF16)
            cp.start()

    def x_copy(way, step, early):
        k = 3 * way + 2 * step - (0 if early else 1)
        return remote(x_out.at[k], x_in.at[k], send_sem.at[4], x_recv.at[k], x_to[way]), k

    def x_go(step, early):
        for way in range(2):
            h = way if early else 1 - way
            d = 2 - step if way == 0 else 2 + step
            v = be[x_at[d], pl.ds(h * HW, HW), :]
            if step == 1 and early:
                cp, k = x_copy(way, 0, True)
                cp.wait_recv()
                v = v + x_in[k].astype(F32)
            cp, k = x_copy(way, step, early)
            x_out[k] = v.astype(BF16)
            cp.start()

    def a_copy(way, kind, e):
        h = 1 - way if kind == 1 else way
        rows = be_fin.at[e, pl.ds(h * HW, HW)]
        return remote(rows, rows, send_sem.at[5], a_recv.at[3 * way + kind], x_to[way])

    def beta_whole():
        for h in range(2):
            cp, early = x_copy(h, 1, True)
            cp.wait_recv()
            cp, late = x_copy(1 - h, 1, False)
            cp.wait_recv()
            rows = pl.ds(h * HW, HW)
            v = be[i, rows, :] + x_in[early].astype(F32) + x_in[late].astype(F32)
            w = wp[rows, pl.ds(pl.multiple_of(i * 256, 256), 256)].astype(F32)
            be_fin[i, rows, :] = (v * w).astype(BF16)
            a_copy(h, 0, i).start()
        for way in range(2):
            a_copy(way, 1, i).start()

    def from_way(way):
        return x_at[3] if way == 0 else x_at[1]

    theta(4)
    y_go(0, True)
    beta(2)
    x_go(0, True)
    beta(1)
    beta(3)
    theta(3)
    theta(5)
    x_go(1, False)
    y_go(1, False)
    theta(2)
    theta(6)
    beta(0)
    y_go(1, True)
    x_go(1, True)
    theta(1)
    theta(7)
    theta(0)
    y_go(2, False)
    y_go(2, True)
    beta_whole()
    y_go(3, False)
    y_go(3, True)
    for way in range(2):
        a_copy(way, 0, from_way(way)).wait_recv()
        a_copy(way, 2, from_way(way)).start()
    for h in range(2):
        cp, late = y_copy(1 - h, 3, False)
        cp.wait_recv()
        cp, early = y_copy(h, 3, True)
        cp.wait_recv()
        rows = pl.ds(h * HD, HD)
        th_fin[rows, :] = th[l, rows, :] + y_in[early].astype(F32) + y_in[late].astype(F32)
    for way in range(2):
        a_copy(way, 1, from_way(way)).wait_recv()
    for way in range(2):
        a_copy(way, 2, x_at[2]).wait_recv()

    remote(c_in, c_in, c_sem.at[2], c_sem.at[0], other).wait_send()
    remote(seven, seven, send_sem.at[0], z_recv.at[0], other).wait_send()
    remote(seven, seven, send_sem.at[1], z_recv.at[0], other).wait_send()
    remote(z_out, z_out, send_sem.at[2], z_recv.at[0], other).wait_send()
    remote(y_out, y_in, send_sem.at[3], z_recv.at[0], other).wait_send()
    remote(x_out, x_in, send_sem.at[4], z_recv.at[0], other).wait_send()
    remote(x_out, x_in, send_sem.at[5], z_recv.at[0], other).wait_send()


def finish(th_ref, be_ref, theta_hbm, beta_hbm, sem):
    copies = [pltpu.make_async_copy(th_ref, theta_hbm, sem.at[4])]
    for e in range(4):
        copies.append(pltpu.make_async_copy(be_ref.at[e], beta_hbm.at[:, pl.ds(e * 256, 256)], sem.at[e]))
    for cp in copies:
        cp.start()
    for cp in copies:
        cp.wait()


def on_device(doc_topics, word_logits, log_norm, tile_doc, tile_word, word_counts):
    n_docs, width = doc_topics.shape
    n_words = word_logits.shape[0]
    slots = tile_doc.shape[0]
    hbm = pl.BlockSpec(memory_space=pltpu.HBM)
    vmem = pl.BlockSpec(memory_space=pltpu.VMEM)
    V, D = pltpu.VMEM, pltpu.SemaphoreType.DMA
    operands = (doc_topics, word_logits, log_norm.reshape(1, width), tile_doc, tile_word, word_counts)
    theta, beta = pl.pallas_call(
        kernel,
        out_shape=(
            jax.ShapeDtypeStruct((n_docs, 128), F32),
            jax.ShapeDtypeStruct((4, n_words, 256), BF16),
        ),
        in_specs=[hbm] * 6,
        out_specs=(vmem, vmem),
        scratch_shapes=[
            V((n_docs, width), BF16),
            V((n_words, width), BF16),
            V((1, width), F32),
            pltpu.SMEM((slots,), jnp.int32),
            pltpu.SMEM((slots,), jnp.int32),
            V(word_counts.shape, jnp.int32),
            V((n_words, width), BF16),
            V((2, 8, WS, DS), BF16),
            V((8, WS, DS), BF16),
            V((8, WS, DS), BF16),
            V((8, WS, DS), BF16),
            V((2, 8, WS, DS), BF16),
            V((n_docs, n_words), BF16),
            V((n_words, n_docs), BF16),
            V((8, n_docs, 128), F32),
            V((14, 2 * DS, 128), BF16),
            V((14, 2 * DS, 128), BF16),
            V((4, n_words, 256), F32),
            V((6, 2 * WS, 256), BF16),
            V((6, 2 * WS, 256), BF16),
            D((7,)),
            D((3,)),
            D((6,)),
            D((1,)),
            D((7,)),
            D((1,)),
            D((14,)),
            D((6,)),
            D((6,)),
            pltpu.SemaphoreType.REGULAR((8,)),
            pltpu.SemaphoreType.REGULAR((2,)),
        ],
        compiler_params=pltpu.CompilerParams(
            collective_id=0, has_side_effects=True, vmem_limit_bytes=40 << 20
        ),
        name="decoder_gradients",
    )(*(pltpu.with_memory_space_constraint(x, pltpu.HBM) for x in operands))
    return pl.pallas_call(
        finish,
        out_shape=(
            jax.ShapeDtypeStruct((n_docs, 128), F32),
            jax.ShapeDtypeStruct((n_words, width), BF16),
        ),
        in_specs=[pl.BlockSpec(memory_space=pl.ANY)] * 2,
        out_specs=(hbm, hbm),
        scratch_shapes=[D((5,))],
        name="write_out",
    )(*(pltpu.with_memory_space_constraint(x, pltpu.VMEM) for x in (theta, beta)))


def solution(mesh):
    placed = (
        P("doc", "topic"),
        P("vocab", "topic"),
        P("topic"),
        P(("doc", "vocab")),
        P(("doc", "vocab")),
        P(("doc", "vocab"), None, None),
    )
    return jax.shard_map(
        on_device,
        mesh=mesh,
        in_specs=placed,
        out_specs=(P("doc", ("topic", "vocab")), P("vocab", "topic")),
        check_vma=False,
    )
```
